32 devices in a mesh: dp: 2 (over x), row: 2 (over core), col: 8 (over z, y).
Axes of the slice: x: 2, y: 2, z: 4, core: 2. Of those that a mesh axis runs over, the one named last changes fastest.
Arguments:
- tokens: bfloat16 [12288, 1024], P(('dp', 'col'), 'row'), may hold values from -6 to 6
- segments: int32 [12, 1024], P(('dp', 'row')), may hold values from 0 to 17, as said below
- attend_gain: bfloat16 [1024], P('row'), may hold values from 0.5 to 1.5
- attend_shift: bfloat16 [1024], P('row'), may hold values from -1.75 to 1.75
- input_weight: bfloat16 [1024, 3, 1024], P('row', None, 'col'), may hold values from -0.1875 to 0.1875
- input_bias: bfloat16 [2, 1024], P(None, 'col'), may hold values from -3 to 3
- output_weight: bfloat16 [1024, 1024], P('col', 'row'), may hold values from -1.5 to 1.5
- output_bias: bfloat16 [1024], P('row'), may hold values from -1.75 to 1.75
- feed_gain: bfloat16 [1024], P('row'), may hold values from 0.5 to 1.5
- feed_shift: bfloat16 [1024], P('row'), may hold values from -1.75 to 1.75
- up_weight: bfloat16 [1024, 4096], P('row', 'col'), may hold values from -0.1875 to 0.1875
- up_bias: bfloat16 [4096], P('col'), may hold values from -1.75 to 1.75
- down_weight: bfloat16 [4096, 1024], P('col', 'row'), may hold values from -0.09375 to 0.09375
- down_bias: bfloat16 [1024], P('row'), may hold values from -1.75 to 1.75
- grad_out: bfloat16 [12288, 1024], P(('dp', 'col'), 'row'), may hold values from -6 to 6
Outputs:
- layer_out: bfloat16 [12288, 1024], P(('dp', 'col'), 'row')
- grad_tokens: float32 [12288, 1024], P(('dp', 'col'), 'row')
- grad_attend_gain: float32 [1024], P('row')
- grad_attend_shift: float32 [1024], P('row')
- grad_input_weight: float32 [1024, 3, 1024], P('row', None, 'col')
- grad_input_bias: float32 [2, 1024], P(None, 'col')
- grad_output_weight: float32 [1024, 1024], P('col', 'row')
- grad_output_bias: float32 [1024], P('row')
- grad_feed_gain: float32 [1024], P('row')
- grad_feed_shift: float32 [1024], P('row')
- grad_up_weight: float32 [1024, 4096], P('row', 'col')
- grad_up_bias: float32 [4096], P('col')
- grad_down_weight: float32 [4096, 1024], P('col', 'row')
- grad_down_bias: float32 [1024], P('row')
The draws below stay inside these ranges and needn't reach their ends.
Inputs may be any that keep to these rules, and one draw needn't show every extreme that they name: `segments`: along each sequence the numbers never fall; documents are numbered 1, 2, 3 in order; every sequence ends in padding marked 0, and 0 appears nowhere else. The first sequence reaches the largest document number.
All inputs are finite; a program needn't handle non-finite values.
Results may differ from the reference program's by a relative error of at most 0.0092.
Values may be sent and summed in bfloat16 or wider, within the bound.
No kernel may reach another device: no remote copies, remote signals or barrier semaphores. Data moves between devices by JAX's collectives and lax.ppermute only.
A program may use at most 192 MiB of HBM per device.

```python
import jax
import jax.numpy as jnp
from jax import lax

D = 1024
H = 16
FF = 4096
LEN = 1024
TOKENS = 12288
SEQS = 12


def draw_segments(key, part):
    shortest = max(LEN * 15 // 256, 1)
    longest = LEN * 25 // 32
    columns = LEN // shortest + 1
    least_padding = LEN // 64 + 1
    first_key, second_key = jax.random.split(key, 2)
    doc_sizes = jax.random.randint(first_key, (SEQS, columns), shortest, longest + 1)
    first_row = (jnp.arange(SEQS) == 0)[:, None]
    doc_sizes = jnp.where(first_row, shortest, doc_sizes)
    doc_ends = jnp.cumsum(doc_sizes, axis=1)
    positions = jnp.arange(LEN)
    numbers = 1 + jnp.sum((positions[None, :, None] >= doc_ends[:, None, :]).astype(jnp.int32), axis=2)
    padding = jax.random.randint(second_key, (SEQS, 1), least_padding, LEN // 4 + 1)
    padding = jnp.where(first_row, least_padding, padding)
    return jnp.where(positions[None, :] >= LEN - padding, 0, numbers).astype(jnp.int32)


def steps_of(stream_key, extent, cuts, smallest, high):
    level, own = 1.0, jax.random.fold_in(stream_key, 6)
    for axis_at, parts in cuts:
        steps = jnp.exp(jax.random.uniform(jax.random.fold_in(own, axis_at), (parts,), jnp.float32, smallest / len(cuts), high / len(cuts)))
        level = level * jnp.repeat(steps, extent[axis_at] // parts).reshape([-1 if axis == axis_at else 1 for axis in range(len(extent))])
    return level


def gaussian(stream_key, extent, width, limit, cuts=(), dtype=jnp.bfloat16):
    drawn = jax.random.normal(stream_key, extent, jnp.float32) * width
    if len(cuts) > 0:
        drawn = steps_of(stream_key, extent, cuts, -0.22, 0.18) * drawn
    return jnp.clip(drawn, min=-limit, max=limit).astype(dtype)


def setup_inputs(seed: int = 0) -> dict:
    key_list = jax.random.split(jax.random.key(seed), 16)
    tokens = gaussian(key_list[0], (TOKENS, D), 1.0, 6.0, ((0, 16), (1, 2)))
    segments = draw_segments(jax.random.fold_in(key_list[15], 71), 0)
    attend_gain = jnp.clip(1.0 + 0.1 * jax.random.normal(key_list[2], (D,), jnp.float32), 0.5, 1.5).astype(jnp.bfloat16)
    attend_shift = gaussian(key_list[3], (D,), 0.3, 1.75, ((0, 2),))
    input_weight = gaussian(key_list[4], (D, 3, D), D ** -0.5, 0.1875, ((0, 2), (2, 8)))
    input_bias = gaussian(key_list[5], (2, D), 0.5, 3.0, ((1, 8),))
    output_weight = gaussian(key_list[6], (D, D), (D // 64) ** -0.5, 1.5, ((0, 8), (1, 2)))
    output_bias = gaussian(key_list[7], (D,), 0.3, 1.75, ((0, 2),))
    feed_gain = jnp.clip(1.0 + 0.1 * jax.random.normal(key_list[8], (D,), jnp.float32), 0.5, 1.5).astype(jnp.bfloat16)
    feed_shift = gaussian(key_list[9], (D,), 0.3, 1.75, ((0, 2),))
    up_weight = gaussian(key_list[10], (D, FF), D ** -0.5, 0.1875, ((0, 2), (1, 8)))
    up_bias = gaussian(key_list[11], (FF,), 0.3, 1.75, ((0, 8),))
    down_weight = gaussian(key_list[12], (FF, D), FF ** -0.5, 0.09375, ((0, 8), (1, 2)))
    down_bias = gaussian(key_list[13], (D,), 0.3, 1.75, ((0, 2),))
    grad_out = gaussian(key_list[14], (TOKENS, D), 1.0, 6.0, ((0, 16), (1, 2)))
    return dict(tokens=tokens, segments=segments, attend_gain=attend_gain, attend_shift=attend_shift, input_weight=input_weight, input_bias=input_bias, output_weight=output_weight, output_bias=output_bias, feed_gain=feed_gain, feed_shift=feed_shift, up_weight=up_weight, up_bias=up_bias, down_weight=down_weight, down_bias=down_bias, grad_out=grad_out)


@jax.custom_vjp
def low(v):
    return lax.optimization_barrier(v.astype(jnp.bfloat16)).astype(jnp.float32)

@jax.custom_vjp
def low_back(v):
    return v

def low_keep(v):
    return (low(v), None)

def low_pass(kept, grad):
    return (grad,)

def back_keep(v):
    return (v, None)

def back_low(kept, grad):
    return (low(grad),)
low.defvjp(low_keep, low_pass)
low_back.defvjp(back_keep, back_low)
epsilon = 1e-05
masked_score = -1000000000.0
highest = lax.Precision.HIGHEST

def normalize(values, gain, shift):
    average = lax.optimization_barrier(jnp.mean(values, axis=-1, keepdims=True))
    square = lax.optimization_barrier(jnp.mean(values * values, axis=-1, keepdims=True))
    inverse = lax.rsqrt(square - average * average + epsilon)
    return (values - average) * inverse * gain + shift

def allowed_pairs(labels):
    positions = jnp.arange(labels.shape[0])
    causal = positions[None, :] <= positions[:, None]
    matching = (labels[:, None] == labels[None, :]) & (labels[:, None] > 0)
    return causal & (matching | (positions[:, None] == positions[None, :]))

def attend(queries, key_rows, values, labels):
    scaling = queries.shape[-1] ** (-0.5)
    scores = low_back(jnp.einsum('qhd,khd->hqk', queries, key_rows, precision=highest) * scaling)
    scores = jnp.where(allowed_pairs(labels)[None], scores, masked_score)
    chances = low(jax.nn.softmax(scores, axis=-1))
    return jnp.einsum('hqk,khd->qhd', chances, values, precision=highest)

def layer(inputs, attend_gain, attend_shift, input_weight, input_bias, output_weight, output_bias, feed_gain, feed_shift, up_weight, up_bias, down_weight, down_bias, labels):
    length, features = inputs.shape
    first = low(normalize(inputs, attend_gain, attend_shift))
    projected = jnp.einsum('td,dke->tke', first, input_weight, precision=highest)
    shifts = jnp.stack([input_bias[0], jnp.zeros_like(input_bias[0]), input_bias[1]])
    projected = low_back(low(projected + shifts))
    heads_all = projected.reshape(length, 3, H, features // H)
    attended = jax.checkpoint(attend)(heads_all[:, 0], heads_all[:, 1], heads_all[:, 2], labels)
    attended = low_back(low(attended.reshape(length, features)))
    middle = inputs + low_back(jnp.dot(attended, output_weight, precision=highest) + output_bias)
    second = low(normalize(middle, feed_gain, feed_shift))
    hidden_pre = low_back(jnp.dot(second, up_weight, precision=highest) + up_bias)
    hidden = low(jax.nn.gelu(hidden_pre, approximate=True))
    return middle + low_back(jnp.dot(hidden, down_weight, precision=highest) + down_bias)

def reference(tokens, segments, attend_gain, attend_shift, input_weight, input_bias, output_weight, output_bias, feed_gain, feed_shift, up_weight, up_bias, down_weight, down_bias, grad_out):
    params = tuple((item.astype(jnp.float32) for item in (attend_gain, attend_shift, input_weight, input_bias, output_weight, output_bias, feed_gain, feed_shift, up_weight, up_bias, down_weight, down_bias)))
    features = tokens.shape[1]
    inputs = tokens.astype(jnp.float32).reshape(SEQS, LEN, features)
    cotangent = grad_out.astype(jnp.float32).reshape(SEQS, LEN, features)

    def one_sequence(totals, packed):
        sequence, labels, pulled_back = packed

        def apply(values, *weights):
            return layer(values, *weights, labels)
        result, puller = jax.vjp(apply, sequence, *params)
        grads = puller(pulled_back)
        return (jax.tree.map(jnp.add, totals, tuple(grads[1:])), (result, grads[0]))
    zeros = tuple((jnp.zeros_like(item) for item in params))
    totals, (results, back_in) = lax.scan(one_sequence, zeros, (inputs, segments, cotangent))
    layer_out = results.reshape(TOKENS, features).astype(jnp.bfloat16)
    grad_tokens = back_in.reshape(TOKENS, features)
    return (layer_out, grad_tokens, totals[0], totals[1], totals[2], totals[3], totals[4], totals[5], totals[6], totals[7], totals[8], totals[9], totals[10], totals[11])
```

```python
import math
from functools import partial

import jax
import jax.numpy as jnp
from jax import lax
from jax.experimental import pallas as pl
from jax.experimental.pallas import tpu as pltpu
from jax.sharding import PartitionSpec as P

HD = 64

epsilon = 1e-05
masked_score = -1000000000.0
low = jnp.bfloat16
full = jnp.float32


def dot_nn(left, right):
    return lax.dot_general(left, right, (((1,), (0,)), ((), ())), preferred_element_type=full)


def dot_nt(left, right):
    return lax.dot_general(left, right, (((1,), (1,)), ((), ())), preferred_element_type=full)


def dot_tn(left, right):
    return lax.dot_general(left, right, (((0,), (0,)), ((), ())), preferred_element_type=full)


def ring_order(count):
    across = {8: 2, 16: 4}.get(count, 1)
    along = count // across
    order = [z * across for z in range(along)]
    for step in range(along):
        z = along - 1 - step
        turn = range(1, across) if step % 2 == 0 else range(across - 1, 0, -1)
        order += [z * across + y for y in turn]
    return order


def shift(values, count, backward):
    order = ring_order(count)
    pairs = [(order[i], order[(i + 1) % count]) for i in range(count)]
    if backward:
        pairs = [(b, a) for a, b in pairs]
    return lax.ppermute(values, "col", pairs)


def ring_gather(ahead, behind, count):
    ahead, behind = [ahead], [behind]
    for _ in range(count - 1):
        ahead.append(shift(ahead[-1], count, False))
        behind.append(shift(behind[-1], count, True))
    return ahead, behind


def ring_scatter(ahead, behind, count):
    one, two = ahead[1 % count].astype(low), behind[1 % count].astype(low)
    for step in range(1, count):
        later = (step + 1) % count
        one = (shift(one, count, False).astype(full) + ahead[later].astype(full)).astype(low)
        two = (shift(two, count, True).astype(full) + behind[later].astype(full)).astype(low)
    return one, two


def swap(values):
    return lax.ppermute(values, "row", [(0, 1), (1, 0)])


def forward_kernel(
    blk, own, low_ref, proj_ref, key_ids, query_ids, out_ref, lse_ref, keys, peak, total, acc
):
    i = pl.program_id(1)

    @pl.when(i == 0)
    def _():
        keys[...] = jnp.transpose(proj_ref[HD : 2 * HD, :])

    start = pl.multiple_of(own + i * blk, blk)
    queries = proj_ref[0:HD, pl.ds(start, blk)] * jnp.asarray(HD**-0.5, low)
    ids = query_ids[...]

    def scores_of(at):
        same = key_ids[pl.ds(at, blk), :] == ids
        return dot_nn(keys[pl.ds(at, blk), :], queries), same

    scores, same = scores_of(start)
    rows = lax.broadcasted_iota(jnp.int32, (blk, blk), 0)
    columns = lax.broadcasted_iota(jnp.int32, (blk, blk), 1)
    scores = jnp.where(same & (rows <= columns), scores, masked_score)
    highest = jnp.max(scores, axis=0, keepdims=True)
    weights = jnp.exp(scores - highest)
    peak[...] = highest
    total[...] = jnp.sum(weights, axis=0, keepdims=True)
    acc[...] = dot_nn(proj_ref[2 * HD : 3 * HD, pl.ds(start, blk)], weights.astype(low))

    def body(j, carry):
        at = pl.multiple_of(j * blk, blk)
        scores, same = scores_of(at)
        scores = jnp.where(same, scores, masked_score)
        before = peak[...]
        highest = jnp.maximum(before, jnp.max(scores, axis=0, keepdims=True))
        shrink = jnp.exp(before - highest)
        weights = jnp.exp(scores - highest)
        peak[...] = highest
        total[...] = total[...] * shrink + jnp.sum(weights, axis=0, keepdims=True)
        acc[...] = acc[...] * shrink + dot_nn(
            proj_ref[2 * HD : 3 * HD, pl.ds(at, blk)], weights.astype(low)
        )
        return carry

    lax.fori_loop(low_ref[i], own // blk + i, body, 0)
    out_ref[...] = (acc[...] / total[...]).astype(low)
    lse_ref[...] = jnp.broadcast_to(peak[...] + jnp.log(total[...]), lse_ref.shape)


def backward_kernel(
    blk,
    own,
    low_ref,
    proj_ref,
    key_ids,
    query_ids,
    out_ref,
    lse_ref,
    grad_ref,
    grad_proj,
    keys,
    values,
    grad_keys,
    grad_values,
    grad_queries,
):
    i = pl.program_id(1)

    @pl.when(i == 0)
    def _():
        keys[...] = jnp.transpose(proj_ref[HD : 2 * HD, :])
        values[...] = jnp.transpose(proj_ref[2 * HD : 3 * HD, :])
        grad_keys[...] = jnp.zeros_like(grad_keys)
        grad_values[...] = jnp.zeros_like(grad_values)
        grad_proj[0:HD, 0:own] = jnp.zeros((HD, own), low)

    start = pl.multiple_of(own + i * blk, blk)
    scaling = jnp.asarray(HD**-0.5, low)
    queries = proj_ref[0:HD, pl.ds(start, blk)] * scaling
    ids = query_ids[...]
    summary = lse_ref[0:1, :]
    grad_out = grad_ref[...]
    against = jnp.sum(
        out_ref[...].astype(full) * grad_out.astype(full), axis=0, keepdims=True
    )

    def block(at, diagonal):
        same = key_ids[pl.ds(at, blk), :] == ids
        if diagonal:
            rows = lax.broadcasted_iota(jnp.int32, (blk, blk), 0)
            columns = lax.broadcasted_iota(jnp.int32, (blk, blk), 1)
            same = same & (rows <= columns)
        scores = dot_nn(keys[pl.ds(at, blk), :], queries)
        chances = jnp.exp(jnp.where(same, scores, masked_score) - summary)
        grad_chances = dot_nn(values[pl.ds(at, blk), :], grad_out)
        grad_values[:, pl.ds(at, blk)] += dot_nt(grad_out, chances.astype(low))
        grad_scores = (chances * (grad_chances - against)).astype(low)
        grad_keys[:, pl.ds(at, blk)] += dot_nt(queries, grad_scores)
        return dot_nn(proj_ref[HD : 2 * HD, pl.ds(at, blk)], grad_scores)

    grad_queries[...] = block(start, True)

    def body(j, carry):
        grad_queries[...] += block(pl.multiple_of(j * blk, blk), False)
        return carry

    lax.fori_loop(low_ref[i], own // blk + i, body, 0)
    grad_proj[0:HD, pl.ds(start, blk)] = (grad_queries[...] * (HD**-0.5)).astype(low)

    @pl.when(i == pl.num_programs(1) - 1)
    def _():
        grad_proj[HD : 2 * HD, :] = grad_keys[...].astype(low)
        grad_proj[2 * HD : 3 * HD, :] = grad_values[...].astype(low)


def attention_specs(blk, own, seen):
    proj = pl.BlockSpec((3 * HD, seen), lambda h, i, s: (h, 0))
    key_ids = pl.BlockSpec((seen, 1), lambda h, i, s: (0, 0))
    query_ids = pl.BlockSpec((1, blk), lambda h, i, s: (0, i))
    out = pl.BlockSpec((HD, blk), lambda h, i, s: (h, i))
    lse = pl.BlockSpec((8, blk), lambda h, i, s: (h, i))
    return proj, key_ids, query_ids, out, lse


def attend_forward(proj, lows, key_ids, query_ids, blk):
    heads, seen = proj.shape[0] // (3 * HD), proj.shape[1]
    own = query_ids.shape[1]
    proj_spec, key_spec, query_spec, out_spec, lse_spec = attention_specs(blk, own, seen)
    return pl.pallas_call(
        partial(forward_kernel, blk, seen - own),
        out_shape=(
            jax.ShapeDtypeStruct((heads * HD, own), low),
            jax.ShapeDtypeStruct((heads * 8, own), full),
        ),
        grid_spec=pltpu.PrefetchScalarGridSpec(
            num_scalar_prefetch=1,
            grid=(heads, own // blk),
            in_specs=[proj_spec, key_spec, query_spec],
            out_specs=[out_spec, lse_spec],
            scratch_shapes=[
                pltpu.VMEM((seen, HD), low),
                pltpu.VMEM((1, blk), full),
                pltpu.VMEM((1, blk), full),
                pltpu.VMEM((HD, blk), full),
            ],
        ),
        cost_estimate=pl.CostEstimate(
            flops=heads * own * 1024 * HD * 8,
            bytes_accessed=heads * HD * seen * 8,
            transcendentals=heads * own * 512,
        ),
        name="attend_forward",
    )(lows, proj, key_ids, query_ids)


def attend_backward(proj, lows, key_ids, query_ids, out, lse, grad, blk):
    heads, seen = proj.shape[0] // (3 * HD), proj.shape[1]
    own = query_ids.shape[1]
    proj_spec, key_spec, query_spec, out_spec, lse_spec = attention_specs(blk, own, seen)
    return pl.pallas_call(
        partial(backward_kernel, blk, seen - own),
        out_shape=jax.ShapeDtypeStruct(proj.shape, low),
        grid_spec=pltpu.PrefetchScalarGridSpec(
            num_scalar_prefetch=1,
            grid=(heads, own // blk),
            in_specs=[proj_spec, key_spec, query_spec, out_spec, lse_spec, out_spec],
            out_specs=proj_spec,
            scratch_shapes=[
                pltpu.VMEM((seen, HD), low),
                pltpu.VMEM((seen, HD), low),
                pltpu.VMEM((HD, seen), full),
                pltpu.VMEM((HD, seen), full),
                pltpu.VMEM((HD, blk), full),
            ],
        ),
        cost_estimate=pl.CostEstimate(
            flops=heads * own * 1024 * HD * 16,
            bytes_accessed=heads * HD * seen * 16,
            transcendentals=heads * own * 512,
        ),
        name="attend_backward",
    )(lows, proj, key_ids, query_ids, out, lse, grad)


def norm_forward(values):
    average = jnp.mean(values, axis=1, keepdims=True)
    square = jnp.mean(values * values, axis=1, keepdims=True)
    inverse = lax.rsqrt(square - average * average + epsilon)
    return (values - average) * inverse, inverse


def halves(array):
    middle = array.shape[0] // 2
    return array[:middle], array[middle:]


def per_device(
    tokens,
    segments,
    attend_gain,
    attend_shift,
    input_weight,
    input_bias,
    output_weight,
    output_bias,
    feed_gain,
    feed_shift,
    up_weight,
    up_bias,
    down_weight,
    down_bias,
    grad_out,
):
    row, col = lax.axis_index("row"), lax.axis_index("col")
    count = lax.axis_size("col")
    own, half = tokens.shape
    length = segments.shape[1]
    blk = min(256, math.gcd(own, length))
    head_width = input_weight.shape[2]
    split_heads = head_width % (2 * HD) == 0
    hidden_width = up_weight.shape[1]
    first_core = row == 0

    def to_core(block):
        one, two = halves(block)
        kept = jnp.where(first_core, one, two)
        sent = jnp.where(first_core, two, one)
        return jnp.concatenate([kept, swap(sent)], axis=1)

    def from_core(block):
        kept, got = block[:, :half], swap(block[:, half:])
        one = jnp.where(first_core, kept, got)
        two = jnp.where(first_core, got, kept)
        return jnp.concatenate([one, two], axis=0)

    def from_other(block):
        block = block.astype(low)
        return swap(jnp.concatenate([block[:, half:], block[:, :half]], axis=1)).astype(full)

    def over_dp(block):
        if lax.axis_size("dp") == 2:
            other = lax.ppermute(block.astype(low), "dp", [(0, 1), (1, 0)])
            return block.astype(low).astype(full) + other.astype(full)
        return lax.psum(block.astype(full), "dp")

    vectors = jnp.stack(
        [attend_gain, attend_shift, output_bias, feed_gain, feed_shift, down_bias]
    )
    vectors = jnp.concatenate([vectors, swap(vectors)], axis=1).astype(full)
    gain_one, shift_one, out_bias, gain_two, shift_two, _ = [vectors[k : k + 1] for k in range(6)]

    needs = [c for c in range(count) if (c * own) % length != 0]
    assert all((c * own) % length <= own for c in needs)
    halo = lax.ppermute(tokens, "col", [(c - 1, c) for c in needs])
    x_own = jnp.concatenate([tokens, swap(tokens)], axis=1).astype(full)
    x_halo = jnp.concatenate([halo, swap(halo)], axis=1).astype(full)

    other_labels = swap(segments)
    labels = jnp.concatenate(
        [
            jnp.where(first_core, segments, other_labels),
            jnp.where(first_core, other_labels, segments),
        ],
        axis=0,
    ).reshape(-1)
    places = jnp.arange(labels.shape[0], dtype=jnp.int32)
    idents = jnp.where(labels > 0, (places // length) * 4096 + labels, -1 - places)
    idents = jnp.concatenate([jnp.full((own,), -(2**30), jnp.int32), idents])
    idents = lax.dynamic_slice_in_dim(idents, col * own, 2 * own, 0)
    key_ids = idents[:, None]
    query_ids = idents[None, own:]
    heads_of_blocks = idents[own::blk]
    lows = jnp.argmax(idents[None, :] == heads_of_blocks[:, None], axis=1).astype(jnp.int32) // blk

    in_block = jnp.transpose(input_weight, (2, 1, 0))
    if split_heads:
        in_block = in_block.reshape(head_width // HD, HD, 3, half).transpose(0, 2, 1, 3)
        in_block = in_block.reshape(3 * head_width, half)
        bias_in = input_bias.reshape(2, head_width // HD, HD)
        bias_in = jnp.stack([bias_in[0], jnp.zeros_like(bias_in[0]), bias_in[1]], axis=1)
        one, two = halves(bias_in.reshape(-1))
        bias_in = jnp.where(first_core, one, two)
        in_block = to_core(in_block)
        out_block = to_core(output_weight)
    up_block = to_core(jnp.transpose(up_weight))
    down_block = to_core(down_weight)
    one, two = halves(up_bias)
    bias_up = jnp.where(first_core, one, two)

    def as_rows(vector):
        return jnp.pad(vector[None, :], ((0, 15), (0, 2 * half - vector.shape[0])))

    def join(ahead, behind):
        parts = []
        for t in range(count):
            parts += [ahead[t], behind[(count - t) % count]]
        return jnp.concatenate(parts, axis=0)

    def part(block, unit):
        mid = unit // 2
        ahead = [block[t * unit : t * unit + mid] for t in range(count)]
        behind = [None] * count
        for t in range(count):
            behind[(count - t) % count] = block[t * unit + mid : (t + 1) * unit]
        return ahead, behind

    up_width = up_block.shape[0]
    extra = [bias_up]
    if split_heads:
        in_width, out_width = in_block.shape[0], out_block.shape[0]
        extra = [bias_in, bias_up]
        packed = [halves(in_block), halves(out_block)]
    else:
        packed = []
    extra = [halves(v) for v in extra]
    packed.append([as_rows(jnp.concatenate([v[k] for v in extra])) for k in range(2)])
    sizes = [p[0].shape[0] for p in packed]
    ahead, behind = ring_gather(
        jnp.concatenate([p[0] for p in packed]), jnp.concatenate([p[1] for p in packed]), count
    )
    groups, at = [], 0
    for size in sizes:
        groups.append(join([a[at : at + size] for a in ahead], [b[at : at + size] for b in behind]))
        at += size
    bias_rows = groups[-1].reshape(2 * count, 16, 2 * half)[:, 0]
    if split_heads:
        in_all, out_all = groups[0], groups[1]
        mid = in_width // 2
        bias_in_all = bias_rows[:, :mid].reshape(-1, 1).astype(full)
        bias_up_all = bias_rows[:, mid : mid + up_width // 2].reshape(1, -1).astype(full)
    else:
        bias_up_all = bias_rows[:, : up_width // 2].reshape(1, -1).astype(full)
        heads = count * head_width // HD
        gathered = lax.all_gather(in_block, "col", axis=0, tiled=True)
        gathered = gathered.reshape(heads, HD, 3, half).transpose(0, 2, 1, 3)
        in_all = to_core(gathered.reshape(heads * 3 * HD, half))
        out_all = to_core(lax.all_gather(output_weight, "col", axis=0, tiled=True))
        bias_all = lax.all_gather(input_bias, "col", axis=1, tiled=True).reshape(2, heads, HD)
        bias_all = jnp.stack([bias_all[0], jnp.zeros_like(bias_all[0]), bias_all[1]], axis=1)
        one, two = halves(bias_all.reshape(-1, 1).astype(full))
        bias_in_all = jnp.where(first_core, one, two)
    up_all = join(*ring_gather(*halves(up_block), count))
    down_all = join(*ring_gather(*halves(down_block), count))

    normed_one, inverse_one = norm_forward(x_own)
    normed_halo, _ = norm_forward(x_halo)
    first = jnp.concatenate([normed_halo, normed_one]) * gain_one + shift_one
    first = first.astype(low)
    proj = (dot_nt(in_all, first) + bias_in_all).astype(low)
    attended, lse = attend_forward(proj, lows, key_ids, query_ids, blk)
    branch = dot_tn(attended, out_all)
    middle = x_own + (branch + from_other(branch) + out_bias)
    normed_two, inverse_two = norm_forward(middle)
    second = (normed_two * gain_two + shift_two).astype(low)
    hidden_pre = dot_nt(second, up_all) + bias_up_all
    gelu_tanh = partial(jax.nn.gelu, approximate=True)
    hidden = gelu_tanh(hidden_pre).astype(low)
    branch = dot_nn(hidden, down_all)
    branch = branch[:, :half] + swap(branch[:, half:].astype(low)).astype(full)
    layer_out = (middle[:, :half] + (branch + down_bias.astype(full))).astype(low)

    grad_full = jnp.concatenate([grad_out, swap(grad_out)], axis=1)
    grad_top = grad_full.astype(full)
    grad_down_bias = jnp.sum(grad_out.astype(full), axis=0)
    grad_down = dot_tn(hidden, grad_full)
    grad_hidden = dot_nt(grad_full, down_all)
    _, gelu_pull = jax.vjp(gelu_tanh, hidden_pre)
    grad_pre = gelu_pull(grad_hidden)[0].astype(low)
    grad_up_bias = jnp.sum(grad_pre.astype(full), axis=0)
    grad_second = dot_nn(grad_pre, up_all)
    grad_up = dot_tn(grad_pre, second)
    grad_second = grad_second + from_other(grad_second)
    scaled = grad_second * gain_two
    grad_middle = grad_top + inverse_two * (
        scaled
        - jnp.mean(scaled, axis=1, keepdims=True)
        - normed_two * jnp.mean(scaled * normed_two, axis=1, keepdims=True)
    )
    grad_feed_gain = jnp.sum(grad_second[:, :half] * normed_two[:, :half], axis=0)
    grad_feed_shift = jnp.sum(grad_second[:, :half], axis=0)
    grad_branch = grad_middle.astype(low)
    grad_output_bias = jnp.sum(grad_branch[:, :half].astype(full), axis=0)
    grad_attended = dot_nt(out_all, grad_branch).astype(low)
    grad_output = dot_nn(attended, grad_branch)
    grad_proj = attend_backward(
        proj, lows, key_ids, query_ids, attended, lse, grad_attended, blk
    )
    grad_bias_in = jnp.sum(grad_proj.astype(full), axis=1)
    grad_input = dot_nn(grad_proj, first)
    grad_first = dot_tn(grad_proj, in_all)
    grad_first = grad_first[:, :half] + swap(grad_first[:, half:].astype(low)).astype(full)
    returned = lax.ppermute(grad_first[:own].astype(low), "col", [(c, c - 1) for c in needs])
    grad_first = grad_first[own:] + returned.astype(full)
    scaled = grad_first * gain_one[:, :half]
    normed_own = normed_one[:, :half]
    sums = jnp.concatenate(
        [
            jnp.sum(scaled, axis=1, keepdims=True),
            jnp.sum(scaled * normed_own, axis=1, keepdims=True),
        ],
        axis=1,
    )
    sums = (sums + swap(sums)) / (2 * half)
    grad_tokens = grad_middle[:, :half] + inverse_one * (
        scaled - sums[:, 0:1] - normed_own * sums[:, 1:2]
    )
    grad_attend_gain = jnp.sum(grad_first * normed_own, axis=0)
    grad_attend_shift = jnp.sum(grad_first, axis=0)

    def finish(one, two):
        return over_dp(from_core(jnp.concatenate([one, two], axis=0)))

    def both(one, two):
        return jnp.concatenate([one, two], axis=0)

    grad_down_weight = finish(*ring_scatter(*part(grad_down, up_width), count))
    grad_up_weight = jnp.transpose(finish(*ring_scatter(*part(grad_up, up_width), count)))

    sum_up = grad_up_bias.reshape(2 * count, up_width // 2)
    if split_heads:
        sum_in = grad_bias_in.reshape(2 * count, in_width // 2)
        sums_rows = jnp.concatenate([sum_in, sum_up], axis=1)
    else:
        sums_rows = sum_up
    used = sums_rows.shape[1]
    sums_rows = jnp.pad(sums_rows[:, None, :], ((0, 0), (0, 15), (0, 2 * half - used)))
    sums_rows = sums_rows.reshape(2 * count * 16, 2 * half)
    parts = [part(sums_rows, 32)]
    if split_heads:
        parts = [part(grad_input, in_width), part(grad_output, out_width)] + parts
    ahead = [jnp.concatenate([p[0][t] for p in parts]) for t in range(count)]
    behind = [jnp.concatenate([p[1][t] for p in parts]) for t in range(count)]
    one, two = ring_scatter(ahead, behind, count)
    pieces, at = [], 0
    for size in sizes:
        pieces.append(jnp.concatenate([one[at : at + size], two[at : at + size]]))
        at += size
    bias_sums = jnp.concatenate([pieces[-1][0:1], pieces[-1][16:17]])
    if split_heads:
        joined = over_dp(from_core(jnp.concatenate(pieces[:2], axis=0)))
        per_core = joined.reshape(2, in_width + out_width, half)
        grad_in = per_core[:, :in_width].reshape(head_width // HD, 3, HD, half)
        grad_input_weight = grad_in.transpose(3, 1, 0, 2).reshape(half, 3, head_width)
        grad_output_weight = per_core[:, in_width:].reshape(head_width, half)
        mid = in_width // 2
        mine_in = bias_sums[:, :mid].reshape(-1)
        mine_up = bias_sums[:, mid : mid + up_width // 2].reshape(-1)
        mine = jnp.concatenate([mine_in, mine_up])
    else:
        heads = count * head_width // HD
        grad_in = from_core(grad_input.astype(low)).reshape(heads, 3, HD, half)
        grad_in = grad_in.transpose(0, 2, 1, 3).reshape(heads * HD, 3, half).astype(full)
        grad_in = lax.psum_scatter(grad_in, "col", scatter_dimension=0, tiled=True)
        grad_input_weight = over_dp(grad_in).transpose(2, 1, 0)
        grad_output_weight = from_core(grad_output.astype(low)).astype(full)
        grad_output_weight = lax.psum_scatter(
            grad_output_weight, "col", scatter_dimension=0, tiled=True
        )
        grad_output_weight = over_dp(grad_output_weight)
        mine = bias_sums[:, : up_width // 2].reshape(-1)
    other = swap(mine)
    mine = over_dp(
        jnp.stack([jnp.where(first_core, mine, other), jnp.where(first_core, other, mine)])
    )
    grad_up_bias = mine[:, -up_width:].reshape(-1)
    if split_heads:
        bias = mine[:, :in_width].reshape(head_width // HD, 3, HD)
        grad_input_bias = jnp.stack([bias[:, 0].reshape(-1), bias[:, 2].reshape(-1)])
    else:
        bias = grad_bias_in.reshape(heads // 2, 3, HD)
        bias = jnp.stack([bias[:, 0].reshape(-1), bias[:, 2].reshape(-1)])
        other = swap(bias)
        bias = jnp.concatenate(
            [jnp.where(first_core, bias, other), jnp.where(first_core, other, bias)], axis=1
        )
        bias = lax.psum_scatter(bias, "col", scatter_dimension=1, tiled=True)
        grad_input_bias = lax.psum(bias, "dp")

    small = jnp.stack(
        [
            grad_attend_gain,
            grad_attend_shift,
            grad_output_bias,
            grad_feed_gain,
            grad_feed_shift,
            grad_down_bias,
        ]
    )
    small = lax.psum(small, ("dp", "col"))
    return (
        layer_out,
        grad_tokens,
        small[0],
        small[1],
        grad_input_weight,
        grad_input_bias,
        grad_output_weight,
        small[2],
        small[3],
        small[4],
        grad_up_weight,
        grad_up_bias,
        grad_down_weight,
        small[5],
    )


def solution(mesh):
    in_specs = (
        P(("dp", "col"), "row"),
        P(("dp", "row"), None),
        P("row"),
        P("row"),
        P("row", None, "col"),
        P(None, "col"),
        P("col", "row"),
        P("row"),
        P("row"),
        P("row"),
        P("row", "col"),
        P("col"),
        P("col", "row"),
        P("row"),
        P(("dp", "col"), "row"),
    )
    out_specs = (
        P(("dp", "col"), "row"),
        P(("dp", "col"), "row"),
        P("row"),
        P("row"),
        P("row", None, "col"),
        P(None, "col"),
        P("col", "row"),
        P("row"),
        P("row"),
        P("row"),
        P("row", "col"),
        P("col"),
        P("col", "row"),
        P("row"),
    )
    return jax.shard_map(
        per_device, mesh=mesh, in_specs=in_specs, out_specs=out_specs, check_vma=False
    )
```

```python
import math
from functools import partial

import jax
import jax.numpy as jnp
from jax import lax
from jax.experimental import pallas as pl
from jax.experimental.pallas import tpu as pltpu
from jax.sharding import PartitionSpec as P

HD = 64

epsilon = 1e-05
masked_score = -1000000000.0
low = jnp.bfloat16
full = jnp.float32


def dot_nn(left, right):
    return lax.dot_general(left, right, (((1,), (0,)), ((), ())), preferred_element_type=full)


def dot_nt(left, right):
    return lax.dot_general(left, right, (((1,), (1,)), ((), ())), preferred_element_type=full)


def dot_tn(left, right):
    return lax.dot_general(left, right, (((0,), (0,)), ((), ())), preferred_element_type=full)


def ring_order(count):
    across = {8: 2, 16: 4}.get(count, 1)
    along = count // across
    order = [z * across for z in range(along)]
    for step in range(along):
        z = along - 1 - step
        turn = range(1, across) if step % 2 == 0 else range(across - 1, 0, -1)
        order += [z * across + y for y in turn]
    return order


def shift(values, count, backward):
    order = ring_order(count)
    pairs = [(order[i], order[(i + 1) % count]) for i in range(count)]
    if backward:
        pairs = [(b, a) for a, b in pairs]
    return lax.ppermute(values, "col", pairs)


def distances(count):
    return sorted(range(count), key=lambda t: (min(t, count - t), t))


def after(values, *others):
    return lax.optimization_barrier((values, *others))[0]


def ring_gather(block, count):
    mid = block.shape[0] // 2
    reach = count // 2
    pieces = {0: [(block, 0)]}
    ahead = behind = block
    for t in range(1, reach):
        ahead, behind = shift(ahead, count, False), shift(behind, count, True)
        pieces[t], pieces[count - t] = [(ahead, 0)], [(behind, 0)]
    ahead, behind = shift(ahead[:mid], count, False), shift(behind[mid:], count, True)
    pieces[reach] = [(ahead, 0), (behind, mid)]
    return pieces


def ring_scatter(blocks, count):
    reach = count // 2
    mid = blocks[0].shape[0] // 2

    def add(block, other):
        return (block.astype(full) + other.astype(full)).astype(low)

    ahead = shift(blocks[reach][:mid].astype(low), count, False)
    behind = shift(blocks[reach][mid:].astype(low), count, True)
    for t in range(reach - 1, 0, -1):
        one, two = blocks[count - t], blocks[t]
        if t == reach - 1:
            one = jnp.concatenate([add(one[:mid], ahead), one[mid:].astype(low)])
            two = jnp.concatenate([two[:mid].astype(low), add(two[mid:], behind)])
        else:
            one, two = add(one, ahead), add(two, behind)
        ahead, behind = shift(one, count, False), shift(two, count, True)
    if reach == 1:
        ahead = jnp.concatenate([ahead, jnp.zeros_like(behind)])
        behind = jnp.concatenate([jnp.zeros_like(ahead[:mid]), behind])
    return blocks[0].astype(full) + ahead.astype(full) + behind.astype(full)


def join(pieces, order, rows):
    sources, places = [], {}
    copies = []
    for number, (first, past) in enumerate(rows):
        for at, t in enumerate(order):
            for block, base in pieces[t]:
                if id(block) not in places:
                    places[id(block)] = len(sources)
                    sources.append(block)
                low_row, high_row = max(first, base), min(past, base + block.shape[0])
                if low_row < high_row:
                    copies.append(
                        (
                            places[id(block)],
                            low_row - base,
                            number,
                            at * (past - first) + low_row - first,
                            high_row - low_row,
                        )
                    )
    width = sources[0].shape[1]

    def kernel(*refs):
        for source, start, number, to, size in copies:
            refs[len(sources) + number][to : to + size, :] = refs[source][start : start + size, :]

    shapes = [
        jax.ShapeDtypeStruct((len(order) * (past - first), width), low) for first, past in rows
    ]
    moved = sum(math.prod(v.shape) for v in shapes) * 4
    return pl.pallas_call(
        kernel,
        out_shape=shapes,
        in_specs=[pl.BlockSpec(memory_space=pltpu.VMEM)] * len(sources),
        out_specs=[pl.BlockSpec(memory_space=pltpu.VMEM)] * len(shapes),
        cost_estimate=pl.CostEstimate(flops=0, bytes_accessed=moved, transcendentals=0),
        name="join",
    )(*sources)


def sum_over(values, axis):
    count = lax.axis_size(axis)
    if count & (count - 1):
        return lax.psum(values, axis)
    step = 1
    while step < count:
        values = values + lax.ppermute(values, axis, [(c, c ^ step) for c in range(count)])
        step *= 2
    return values


def swap(values):
    return lax.ppermute(values, "row", [(0, 1), (1, 0)])


def masks_of(blk, own, key_ids, query_ids, i):
    ids = query_ids[:, i * blk : (i + 1) * blk]

    def mask(at, diagonal):
        same = key_ids[pl.ds(at, blk), :] == ids
        if diagonal:
            rows = lax.broadcasted_iota(jnp.int32, (blk, blk), 0)
            columns = lax.broadcasted_iota(jnp.int32, (blk, blk), 1)
            same = same & (rows <= columns)
        return same

    return mask


def forward_kernel(blk, own, group, low_ref, proj_ref, key_ids, query_ids, out_ref, lse_ref, keys):
    for g in range(group):
        keys[g] = jnp.transpose(proj_ref[(3 * g + 1) * HD : (3 * g + 2) * HD, :])

    for i in range(query_ids.shape[1] // blk):
        mask = masks_of(blk, own, key_ids, query_ids, i)
        start = own + i * blk
        queries = [
            proj_ref[3 * g * HD : (3 * g + 1) * HD, start : start + blk]
            * jnp.asarray(HD**-0.5, low)
            for g in range(group)
        ]

        def values(g, at):
            return proj_ref[(3 * g + 2) * HD : (3 * g + 3) * HD, pl.ds(at, blk)]

        allowed = mask(start, True)
        carry = []
        for g in range(group):
            scores = dot_nn(keys[g, pl.ds(start, blk), :], queries[g])
            scores = jnp.where(allowed, scores, masked_score)
            highest = jnp.max(scores, axis=0, keepdims=True)
            weights = jnp.exp(scores - highest)
            total = jnp.sum(weights, axis=0, keepdims=True)
            carry.append((highest, total, dot_nn(values(g, start), weights.astype(low))))

        def body(j, carry):
            at = pl.multiple_of(j * blk, blk)
            allowed = mask(at, False)
            later = []
            for g, (before, total, acc) in enumerate(carry):
                scores = dot_nn(keys[g, pl.ds(at, blk), :], queries[g])
                scores = jnp.where(allowed, scores, masked_score)
                highest = jnp.maximum(before, jnp.max(scores, axis=0, keepdims=True))
                shrink = jnp.exp(before - highest)
                weights = jnp.exp(scores - highest)
                total = total * shrink + jnp.sum(weights, axis=0, keepdims=True)
                acc = acc * shrink + dot_nn(values(g, at), weights.astype(low))
                later.append((highest, total, acc))
            return tuple(later)

        carry = lax.fori_loop(low_ref[i], own // blk + i, body, tuple(carry))
        for g, (highest, total, acc) in enumerate(carry):
            here = slice(i * blk, (i + 1) * blk)
            out_ref[g * HD : (g + 1) * HD, here] = (acc / total).astype(low)
            lse_ref[g * 8 : g * 8 + 1, here] = highest + jnp.log(total)


def backward_kernel(
    blk,
    own,
    group,
    low_ref,
    proj_ref,
    key_ids,
    query_ids,
    out_ref,
    lse_ref,
    grad_ref,
    grad_proj,
    keys,
    values,
    grad_keys,
    grad_values,
):
    for g in range(group):
        keys[g] = jnp.transpose(proj_ref[(3 * g + 1) * HD : (3 * g + 2) * HD, :])
        values[g] = jnp.transpose(proj_ref[(3 * g + 2) * HD : (3 * g + 3) * HD, :])
        grad_proj[3 * g * HD : (3 * g + 1) * HD, 0:own] = jnp.zeros((HD, own), low)
    grad_keys[...] = jnp.zeros_like(grad_keys)
    grad_values[...] = jnp.zeros_like(grad_values)

    for i in range(query_ids.shape[1] // blk):
        mask = masks_of(blk, own, key_ids, query_ids, i)
        start = own + i * blk
        here = slice(i * blk, (i + 1) * blk)
        queries, against, grads, summary = [], [], [], []
        for g in range(group):
            head = slice(g * HD, (g + 1) * HD)
            queries.append(
                proj_ref[3 * g * HD : (3 * g + 1) * HD, start : start + blk]
                * jnp.asarray(HD**-0.5, low)
            )
            grads.append(grad_ref[head, here])
            product = out_ref[head, here].astype(full) * grads[g].astype(full)
            against.append(jnp.sum(product, axis=0, keepdims=True))
            summary.append(lse_ref[g * 8 : g * 8 + 1, here])

        def blocks(at, diagonal):
            allowed = mask(at, diagonal)
            found = []
            for g in range(group):
                scores = dot_nn(keys[g, pl.ds(at, blk), :], queries[g])
                chances = jnp.exp(jnp.where(allowed, scores, masked_score) - summary[g])
                grad_chances = dot_nn(values[g, pl.ds(at, blk), :], grads[g])
                grad_values[g, :, pl.ds(at, blk)] += dot_nt(grads[g], chances.astype(low))
                grad_scores = (chances * (grad_chances - against[g])).astype(low)
                grad_keys[g, :, pl.ds(at, blk)] += dot_nt(queries[g], grad_scores)
                rows = proj_ref[(3 * g + 1) * HD : (3 * g + 2) * HD, pl.ds(at, blk)]
                found.append(dot_nn(rows, grad_scores))
            return found

        def body(j, carry):
            found = blocks(pl.multiple_of(j * blk, blk), False)
            return tuple(a + b for a, b in zip(carry, found))

        grad_queries = lax.fori_loop(
            low_ref[i], own // blk + i, body, tuple(blocks(start, True))
        )
        for g in range(group):
            grad_proj[3 * g * HD : (3 * g + 1) * HD, start : start + blk] = (
                grad_queries[g] * (HD**-0.5)
            ).astype(low)

    for g in range(group):
        grad_proj[(3 * g + 1) * HD : (3 * g + 2) * HD, :] = grad_keys[g].astype(low)
        grad_proj[(3 * g + 2) * HD : (3 * g + 3) * HD, :] = grad_values[g].astype(low)


def attention_specs(group, own, seen):
    proj = pl.BlockSpec((group * 3 * HD, seen), lambda h, s: (h, 0))
    key_ids = pl.BlockSpec((seen, 1), lambda h, s: (0, 0))
    query_ids = pl.BlockSpec((1, own), lambda h, s: (0, 0))
    out = pl.BlockSpec((group * HD, own), lambda h, s: (h, 0))
    lse = pl.BlockSpec((group * 8, own), lambda h, s: (h, 0))
    return proj, key_ids, query_ids, out, lse


def attend_forward(proj, lows, key_ids, query_ids, blk):
    heads, seen = proj.shape[0] // (3 * HD), proj.shape[1]
    own = query_ids.shape[1]
    group = 2 if heads % 2 == 0 else 1
    proj_spec, key_spec, query_spec, out_spec, lse_spec = attention_specs(group, own, seen)
    return pl.pallas_call(
        partial(forward_kernel, blk, seen - own, group),
        out_shape=(
            jax.ShapeDtypeStruct((heads * HD, own), low),
            jax.ShapeDtypeStruct((heads * 8, own), full),
        ),
        grid_spec=pltpu.PrefetchScalarGridSpec(
            num_scalar_prefetch=1,
            grid=(heads // group,),
            in_specs=[proj_spec, key_spec, query_spec],
            out_specs=[out_spec, lse_spec],
            scratch_shapes=[pltpu.VMEM((group, seen, HD), low)],
        ),
        cost_estimate=pl.CostEstimate(
            flops=heads * own * 1024 * HD * 8,
            bytes_accessed=heads * HD * seen * 8,
            transcendentals=heads * own * 512,
        ),
        name="attend_forward",
    )(lows, proj, key_ids, query_ids)


def attend_backward(proj, lows, key_ids, query_ids, out, lse, grad, blk):
    heads, seen = proj.shape[0] // (3 * HD), proj.shape[1]
    own = query_ids.shape[1]
    group = 2 if heads % 2 == 0 else 1
    proj_spec, key_spec, query_spec, out_spec, lse_spec = attention_specs(group, own, seen)
    return pl.pallas_call(
        partial(backward_kernel, blk, seen - own, group),
        out_shape=jax.ShapeDtypeStruct(proj.shape, low),
        grid_spec=pltpu.PrefetchScalarGridSpec(
            num_scalar_prefetch=1,
            grid=(heads // group,),
            in_specs=[proj_spec, key_spec, query_spec, out_spec, lse_spec, out_spec],
            out_specs=proj_spec,
            scratch_shapes=[
                pltpu.VMEM((group, seen, HD), low),
                pltpu.VMEM((group, seen, HD), low),
                pltpu.VMEM((group, HD, seen), full),
                pltpu.VMEM((group, HD, seen), full),
            ],
        ),
        cost_estimate=pl.CostEstimate(
            flops=heads * own * 1024 * HD * 16,
            bytes_accessed=heads * HD * seen * 16,
            transcendentals=heads * own * 512,
        ),
        name="attend_backward",
    )(lows, proj, key_ids, query_ids, out, lse, grad)


def norm_forward(values):
    average = jnp.mean(values, axis=1, keepdims=True)
    square = jnp.mean(values * values, axis=1, keepdims=True)
    inverse = lax.rsqrt(square - average * average + epsilon)
    return (values - average) * inverse, inverse


def halves(array):
    middle = array.shape[0] // 2
    return array[:middle], array[middle:]


def per_device(
    tokens,
    segments,
    attend_gain,
    attend_shift,
    input_weight,
    input_bias,
    output_weight,
    output_bias,
    feed_gain,
    feed_shift,
    up_weight,
    up_bias,
    down_weight,
    down_bias,
    grad_out,
):
    row, col = lax.axis_index("row"), lax.axis_index("col")
    count = lax.axis_size("col")
    own, half = tokens.shape
    seqs, length = segments.shape
    blk = min(256, math.gcd(own, length))
    head_width = input_weight.shape[2]
    split_heads = head_width % (2 * HD) == 0
    first_core = row == 0
    order = distances(count)
    parts = order[: count // 2], order[count // 2 :]

    def mine_and_other(block):
        rows = block.shape[0] // 2
        block = block.reshape(2, rows, *block.shape[1:])
        return (
            lax.dynamic_index_in_dim(block, row, 0, False),
            lax.dynamic_index_in_dim(block, 1 - row, 0, False),
        )

    def by_core(kept, got):
        return jnp.concatenate(
            [jnp.where(first_core, kept, got), jnp.where(first_core, got, kept)], axis=0
        )

    def from_core(block):
        return by_core(block[:, :half], swap(block[:, half:]))

    def to_core(block):
        kept, sent = mine_and_other(block)
        return jnp.concatenate([kept, swap(sent)], axis=1)

    def from_other(block):
        block = block.astype(low)
        return swap(jnp.concatenate([block[:, half:], block[:, :half]], axis=1)).astype(full)

    def over_dp(block):
        if lax.axis_size("dp") == 2:
            block = block.astype(low)
            other = lax.ppermute(block, "dp", [(0, 1), (1, 0)])
            return block.astype(full) + other.astype(full)
        return lax.psum(block.astype(full), "dp")

    vectors = jnp.stack(
        [attend_gain, attend_shift, output_bias, feed_gain, feed_shift, down_bias]
    )
    labels = segments.astype(low).reshape(-1, half)
    small = jnp.concatenate([vectors, labels], axis=0)
    bias_up = mine_and_other(up_bias)[0]
    up_width = bias_up.shape[0]
    if split_heads:
        in_block = jnp.transpose(input_weight, (2, 1, 0))
        in_block = in_block.reshape(head_width // HD, HD, 3, half).transpose(0, 2, 1, 3)
        in_kept, in_sent = mine_and_other(in_block.reshape(3 * head_width, half))
        out_kept, out_sent = mine_and_other(output_weight)
        in_width, out_width = in_kept.shape[0], out_kept.shape[0]
        got = swap(jnp.concatenate([in_sent, out_sent, small], axis=0))
        weights = jnp.concatenate(
            [
                jnp.concatenate([in_kept, out_kept], axis=0),
                got[: in_width + out_width],
            ],
            axis=1,
        )
        other_small = got[in_width + out_width :]
        bias_in = input_bias.reshape(2, head_width // HD, HD)
        bias_in = jnp.stack([bias_in[0], jnp.zeros_like(bias_in[0]), bias_in[1]], axis=1)
        bias_in = mine_and_other(bias_in.reshape(-1))[0]
        bias_row = jnp.concatenate([bias_in, bias_up])
    else:
        in_width = out_width = 0
        weights = jnp.zeros((0, 2 * half), low)
        other_small = swap(small)
        bias_row = bias_up
    bias_rows = 32
    bias_row = jnp.pad(bias_row[None], ((0, bias_rows - 1), (0, 2 * half - bias_row.shape[0])))
    block = jnp.concatenate([weights, bias_row], axis=0)
    pieces = ring_gather(block, count)
    edges = [(0, in_width), (in_width, in_width + out_width)] if split_heads else []
    edges += [(in_width + out_width, in_width + out_width + bias_rows)]
    joined = [join(pieces, part, edges) for part in parts]
    last = pieces[count // 2 - 1][0][0]

    needs = [c for c in range(count) if (c * own) % length != 0]
    assert all((c * own) % length <= own for c in needs)
    halo = lax.ppermute(tokens, "col", [(c - 1, c) for c in needs])
    x_own = jnp.concatenate([tokens, swap(tokens)], axis=1).astype(full)
    x_halo = jnp.concatenate([halo, swap(halo)], axis=1).astype(full)
    vectors = jnp.concatenate([vectors, other_small[:6]], axis=1).astype(full)
    gain_one, shift_one, out_bias, gain_two, shift_two, _ = [vectors[k : k + 1] for k in range(6)]
    labels = by_core(labels, other_small[6:]).reshape(-1).astype(jnp.int32)
    places = jnp.arange(labels.shape[0], dtype=jnp.int32)
    idents = jnp.where(labels > 0, (places // length) * 4096 + labels, -1 - places)
    idents = jnp.concatenate([jnp.full((own,), -(2**30), jnp.int32), idents])
    idents = lax.dynamic_slice_in_dim(idents, col * own, 2 * own, 0)
    key_ids = idents[:, None]
    query_ids = idents[None, own:]
    heads_of_blocks = idents[own::blk]
    lows = jnp.argmax(idents[None, :] == heads_of_blocks[:, None], axis=1).astype(jnp.int32) // blk

    up_weight, down_weight = after((up_weight, down_weight), block)
    up_kept, up_sent = mine_and_other(jnp.transpose(up_weight))
    down_kept, down_sent = mine_and_other(down_weight)
    got = swap(jnp.concatenate([up_sent, down_sent], axis=0))
    up_block = jnp.concatenate([up_kept, got[:up_width]], axis=1)
    down_block = jnp.concatenate([down_kept, got[up_width:]], axis=1)
    up_pieces = ring_gather(after(up_block, last), count)
    last = up_pieces[count // 2 - 1][0][0]
    down_pieces = ring_gather(after(down_block, last), count)
    up = [join(up_pieces, part, [(0, up_width)])[0] for part in parts]
    down = [join(down_pieces, part, [(0, up_width)])[0] for part in parts]
    bias_rows_of = [v[-1].reshape(-1, bias_rows, 2 * half)[:, 0] for v in joined]
    if split_heads:
        into, out = [v[0] for v in joined], [v[1] for v in joined]
        bias_in = [v[:, :in_width].reshape(-1, 1).astype(full) for v in bias_rows_of]
        bias_up = [v[:, in_width : in_width + up_width] for v in bias_rows_of]
    else:
        heads = count * head_width // HD
        gathered = jnp.transpose(input_weight, (2, 1, 0))
        gathered = lax.all_gather(gathered, "col", axis=0, tiled=True)
        gathered = gathered.reshape(heads, HD, 3, half).transpose(0, 2, 1, 3)
        into = halves(to_core(gathered.reshape(heads * 3 * HD, half)))
        out = halves(to_core(lax.all_gather(output_weight, "col", axis=0, tiled=True)))
        bias_all = lax.all_gather(input_bias, "col", axis=1, tiled=True).reshape(2, heads, HD)
        bias_all = jnp.stack([bias_all[0], jnp.zeros_like(bias_all[0]), bias_all[1]], axis=1)
        bias_in = halves(mine_and_other(bias_all.reshape(-1, 1).astype(full))[0])
        bias_up = [v[:, :up_width] for v in bias_rows_of]
    bias_up = [v.reshape(1, -1).astype(full) for v in bias_up]

    both = range(2)
    near, far = 0, 1
    fixed = lax.optimization_barrier
    normed_one, inverse_one = norm_forward(x_own)
    normed_halo, _ = norm_forward(x_halo)
    first = jnp.concatenate([normed_halo, normed_one]) * gain_one + shift_one
    first = fixed(first.astype(low))
    proj, attended, lse = [], [], []
    for k in both:
        proj.append((dot_nt(into[k], first) + bias_in[k]).astype(low))
        result = attend_forward(proj[k], lows, key_ids, query_ids, blk)
        attended.append(result[0])
        lse.append(result[1])
    branch = sum(dot_tn(attended[k], out[k]) for k in both)
    middle = x_own + (branch + from_other(branch) + out_bias)
    normed_two, inverse_two = norm_forward(middle)
    second = fixed((normed_two * gain_two + shift_two).astype(low))
    hidden, slope = [], []
    for k in both:
        pre = dot_nt(second, up[k]) + bias_up[k]
        value, pull = jax.vjp(partial(jax.nn.gelu, approximate=True), pre)
        value, rate = fixed((value.astype(low), pull(jnp.ones_like(pre))[0]))
        hidden.append(value)
        slope.append(rate)
    grad_full = fixed(jnp.concatenate([grad_out, swap(grad_out)], axis=1))
    grad_down = [None, None]
    for k in (far, near):
        grad_down[k] = dot_tn(hidden[k], grad_full).astype(low)
    branch = sum(dot_nn(hidden[k], down[k]) for k in both)
    branch = branch[:, :half] + swap(branch[:, half:].astype(low)).astype(full)
    layer_out = (middle[:, :half] + (branch + down_bias.astype(full))).astype(low)

    grad_pre, grad_up, grad_up_bias = [None, None], [None, None], [None, None]
    for k in (far, near):
        grad_pre[k] = fixed((dot_nt(grad_full, down[k]) * slope[k]).astype(low))
        grad_up_bias[k] = jnp.sum(grad_pre[k].astype(full), axis=0)
        grad_up[k] = dot_tn(grad_pre[k], second).astype(low)
    grad_second = sum(dot_nn(grad_pre[k], up[k]) for k in both)
    grad_second = grad_second + from_other(grad_second)
    scaled = grad_second * gain_two
    grad_middle = grad_full.astype(full) + inverse_two * (
        scaled
        - jnp.mean(scaled, axis=1, keepdims=True)
        - normed_two * jnp.mean(scaled * normed_two, axis=1, keepdims=True)
    )
    grad_branch = fixed(grad_middle.astype(low))
    grad_output, grad_proj, grad_input = [None, None], [None, None], [None, None]
    grad_bias_in = [None, None]
    for k in (far, near):
        grad_output[k] = dot_nn(attended[k], grad_branch).astype(low)
    for k in (far, near):
        grad_attended = dot_nt(out[k], grad_branch).astype(low)
        grad_proj[k] = attend_backward(
            proj[k], lows, key_ids, query_ids, attended[k], lse[k], grad_attended, blk
        )
        grad_bias_in[k] = jnp.sum(grad_proj[k].astype(full), axis=1)
        grad_input[k] = dot_nn(grad_proj[k], first).astype(low)

    def split(blocks, unit):
        found = {}
        for part, block in zip(parts, blocks):
            for at, t in enumerate(part):
                found[t] = block[at * unit : (at + 1) * unit]
        return found

    def beside(*found):
        return {t: jnp.concatenate([f[t] for f in found], axis=0) for t in range(count)}

    total = ring_scatter(split(grad_down, up_width), count)
    grad_down_weight = over_dp(from_core(total.astype(low)))
    blocks = split(grad_up, up_width)
    if split_heads:
        blocks = beside(blocks, split(grad_output, out_width))
    total = from_core(ring_scatter(blocks, count).astype(low))
    total = over_dp(total).reshape(2, -1, half)
    grad_up_weight = jnp.transpose(total[:, :up_width].reshape(-1, half))
    grad_output_weight = total[:, up_width:].reshape(-1, half)

    rows = []
    for k in both:
        row_up = grad_up_bias[k].reshape(-1, up_width)
        if split_heads:
            row_up = jnp.concatenate([grad_bias_in[k].reshape(-1, in_width), row_up], axis=1)
        used = row_up.shape[1]
        row_up = jnp.pad(row_up[:, None], ((0, 0), (0, bias_rows - 1), (0, 2 * half - used)))
        rows.append(row_up.reshape(-1, 2 * half).astype(low))
    blocks = split(rows, bias_rows)
    if split_heads:
        blocks = beside(split(grad_input, in_width), blocks)
    total = ring_scatter(blocks, count).astype(low)
    bias_sums = total[in_width, : in_width + up_width]
    if split_heads:
        total = over_dp(from_core(total[:in_width]))
        total = total.reshape(head_width // HD, 3, HD, half)
        grad_input_weight = total.transpose(3, 1, 0, 2).reshape(half, 3, head_width)
    else:
        total = from_core(jnp.concatenate(grad_input)).reshape(heads, 3, HD, half)
        total = total.transpose(0, 2, 1, 3).reshape(heads * HD, 3, half).astype(full)
        total = lax.psum_scatter(total, "col", scatter_dimension=0, tiled=True)
        grad_input_weight = over_dp(total).transpose(2, 1, 0)
        total = from_core(jnp.concatenate(grad_output)).astype(full)
        total = lax.psum_scatter(total, "col", scatter_dimension=0, tiled=True)
        grad_output_weight = over_dp(total)
    bias_sums = over_dp(by_core(bias_sums[None], swap(bias_sums[None])))
    if split_heads:
        bias = bias_sums[:, :in_width].reshape(head_width // HD, 3, HD)
        grad_input_bias = jnp.stack([bias[:, 0].reshape(-1), bias[:, 2].reshape(-1)])
    else:
        bias = jnp.concatenate(grad_bias_in).reshape(heads // 2, 3, HD)
        bias = jnp.stack([bias[:, 0].reshape(-1), bias[:, 2].reshape(-1)], axis=1)
        bias = by_core(bias, swap(bias))
        bias = lax.psum_scatter(bias, "col", scatter_dimension=0, tiled=True)
        grad_input_bias = lax.psum(bias, "dp").T

    grad_first = sum(dot_tn(grad_proj[k], into[k]) for k in both)
    grad_first = grad_first[:, :half] + swap(grad_first[:, half:].astype(low)).astype(full)
    returned = lax.ppermute(grad_first[:own].astype(low), "col", [(c, c - 1) for c in needs])
    grad_first = grad_first[own:] + returned.astype(full)
    scaled = grad_first * gain_one[:, :half]
    normed_own = normed_one[:, :half]
    sums = jnp.concatenate(
        [
            jnp.sum(scaled, axis=1, keepdims=True),
            jnp.sum(scaled * normed_own, axis=1, keepdims=True),
        ],
        axis=1,
    )
    sums = (sums + swap(sums)) / (2 * half)
    grad_tokens = grad_middle[:, :half] + inverse_one * (
        scaled - sums[:, 0:1] - normed_own * sums[:, 1:2]
    )
    small = jnp.stack(
        [
            jnp.sum(grad_first * normed_own, axis=0),
            jnp.sum(grad_first, axis=0),
            jnp.sum(grad_branch[:, :half].astype(full), axis=0),
            jnp.sum(grad_second[:, :half] * normed_two[:, :half], axis=0),
            jnp.sum(grad_second[:, :half], axis=0),
            jnp.sum(grad_out.astype(full), axis=0),
        ]
    )
    small = sum_over(sum_over(small, "dp"), "col")
    return (
        layer_out,
        grad_tokens,
        small[0],
        small[1],
        grad_input_weight,
        grad_input_bias,
        grad_output_weight,
        small[2],
        small[3],
        small[4],
        grad_up_weight,
        bias_sums[:, in_width:].reshape(-1),
        grad_down_weight,
        small[5],
    )


def solution(mesh):
    in_specs = (
        P(("dp", "col"), "row"),
        P(("dp", "row"), None),
        P("row"),
        P("row"),
        P("row", None, "col"),
        P(None, "col"),
        P("col", "row"),
        P("row"),
        P("row"),
        P("row"),
        P("row", "col"),
        P("col"),
        P("col", "row"),
        P("row"),
        P(("dp", "col"), "row"),
    )
    out_specs = (
        P(("dp", "col"), "row"),
        P(("dp", "col"), "row"),
        P("row"),
        P("row"),
        P("row", None, "col"),
        P(None, "col"),
        P("col", "row"),
        P("row"),
        P("row"),
        P("row"),
        P("row", "col"),
        P("col"),
        P("col", "row"),
        P("row"),
    )
    return jax.shard_map(
        per_device, mesh=mesh, in_specs=in_specs, out_specs=out_specs, check_vma=False
    )
```
